32 devices in a mesh: region: 2 (over x), owner: 16 (over z, y, core).
Axes of the slice: x: 2, y: 2, z: 4, core: 2. Of those that a mesh axis runs over, the one named last changes fastest.
Arguments:
- voxels: bfloat16 [2, 16, 1, 256, 1024], P('region', 'owner'), may hold values from -6 to 6
- norm_gain: float32 [1024], replicated, may hold values from 0.5 to 1.5
- qkv_weight: bfloat16 [1024, 3072], P(('region', 'owner')), may hold values from -0.14453125 to 0.14453125
- out_weight: bfloat16 [1024, 1024], P(('region', 'owner')), may hold values from -0.1875 to 0.1875
- neighbours: int32 [2, 16, 1, 8], P('region', 'owner'), may hold values from -1 to 31, as said below
Outputs:
- attended_voxels: bfloat16 [2, 16, 1, 256, 1024], P('region', 'owner')
The draws below stay inside these ranges and needn't reach their ends.
Inputs may be any that keep to these rules, and one draw needn't show every extreme that they name: `neighbours`: each entry is -1 or the number (r * 16 + o) + c of a block c held by the device at region r and owner o, where r and o each differ by at most one from those of the list's own block; a list never names its own block and names no block twice.
All inputs are finite; a program needn't handle non-finite values.
Results may differ from the reference program's by a relative error of at most 0.0057.
Values may be sent and summed in bfloat16 or wider, within the bound.
A program may use at most 64 MiB of HBM per device.

```python
import jax
import jax.numpy as jnp
from jax import lax

D = 1024
HEADS = 16
HEAD_DIM = 64
S = 256
CAP = 1
NBR = 8
REGIONS = 2
OWNERS = 16


def common_direction(key):
    base = jax.random.normal(jax.random.fold_in(key, 501), (D,), jnp.float32)
    base = jnp.clip(base, -2.2, 2.2)
    base = base - jnp.mean(base)
    return base / jnp.sqrt(jnp.mean(base * base))


def draw_voxels(key, part):
    shape = (REGIONS, OWNERS, CAP, S, D)
    return jax.random.truncated_normal(jax.random.fold_in(key, 504), -6.0, 6.0, shape, jnp.float32).astype(jnp.bfloat16)


def draw_qkv_weight(key, part):
    direction = common_direction(key)
    random_part = jax.random.truncated_normal(jax.random.fold_in(key, 511), -4.0, 4.0, (D, 3 * D), jnp.float32) * D ** (-0.5)
    levels = jax.random.permutation(jax.random.fold_in(key, 512), HEADS).astype(jnp.float32) / (HEADS - 1)
    strength = 7.0 ** levels
    signs = jnp.where(jax.random.bernoulli(jax.random.fold_in(key, 513), 0.5, (HEADS, HEAD_DIM)), 1.0, -1.0)
    pattern = (strength[:, None] * signs).reshape(D) / D
    aligned = direction[:, None] * pattern[None, :]
    blank = jnp.zeros((D, D), jnp.float32)
    return (random_part + jnp.concatenate([aligned, aligned, blank], axis=1)).astype(jnp.bfloat16)


def draw_neighbours(key, part):
    candidate_count = 9 * CAP
    region_ids = jnp.arange(REGIONS, dtype=jnp.int32)[:, None, None, None]
    owner_ids = jnp.arange(OWNERS, dtype=jnp.int32)[None, :, None, None]
    slot_ids = jnp.arange(CAP, dtype=jnp.int32)[None, None, :, None]
    candidate_ids = jnp.arange(candidate_count, dtype=jnp.int32)[None, None, None, :]
    noise = jax.random.randint(jax.random.fold_in(key, 11), (REGIONS, OWNERS, CAP, candidate_count), 0, 1 << 20)
    ranking = noise * 64 + candidate_ids
    ranking = jnp.where(candidate_ids == 4 * CAP + slot_ids, 1 << 30, ranking)
    chosen = jnp.argsort(ranking, axis=-1, stable=True)[..., :NBR].astype(jnp.int32)
    device_pos = chosen // CAP
    other_slot = chosen % CAP
    far_region = region_ids + device_pos // 3 - 1
    far_owner = owner_ids + device_pos % 3 - 1
    inside = (far_region >= 0) & (far_region < REGIONS) & (far_owner >= 0) & (far_owner < OWNERS)
    keeping = jax.random.randint(jax.random.fold_in(key, 12), (REGIONS, OWNERS, CAP, NBR), 0, 10) < 7
    numbers = (far_region * OWNERS + far_owner) * CAP + other_slot
    return jnp.where(inside & keeping, numbers, -1).astype(jnp.int32)


def level_of(rng, extent, cuts, least, high):
    loudness, own = 1.0, jax.random.fold_in(rng, 6)
    for axis_at, blocks in cuts:
        draws = jnp.exp(jax.random.uniform(jax.random.fold_in(own, axis_at), (blocks,), jnp.float32, least / len(cuts), high / len(cuts)))
        loudness = loudness * jnp.repeat(draws, extent[axis_at] // blocks).reshape([-1 if axis == axis_at else 1 for axis in range(len(extent))])
    return loudness


def centred(key, dims, deviation, most, cuts=(), held_as=jnp.bfloat16):
    values = jax.random.normal(key, dims, jnp.float32) * deviation
    if len(cuts) > 0:
        values = level_of(key, dims, cuts, -0.22, 0.18) * values
    return jnp.clip(values, min=-most, max=most).astype(held_as)


def setup_inputs(seed: int = 0) -> dict:
    seeds = jax.random.split(jax.random.key(seed), 6)
    return {
        "voxels": draw_voxels(jax.random.fold_in(seeds[5], 71), 0),
        "norm_gain": jnp.clip(1.0 + 0.1 * jax.random.normal(seeds[1], (D,), jnp.float32), 0.5, 1.5),
        "qkv_weight": draw_qkv_weight(jax.random.fold_in(seeds[5], 71), 0),
        "out_weight": centred(seeds[3], (D, D), D ** -0.5, 0.1875, ((0, 32),)),
        "neighbours": draw_neighbours(jax.random.fold_in(seeds[5], 71), 0),
    }


def layer_norm(inputs, norm_gain):
    widened = inputs.astype(jnp.float32)
    average = lax.optimization_barrier(jnp.mean(widened, axis=-1, keepdims=True))
    spread = lax.optimization_barrier(jnp.mean((widened - average) ** 2, axis=-1, keepdims=True))
    return ((widened - average) * lax.rsqrt(spread + 1e-06) * norm_gain).astype(jnp.bfloat16)

def reference(voxels, norm_gain, qkv_weight, out_weight, neighbours):
    model_width = voxels.shape[-1]
    block_size = voxels.shape[3]
    flat_tokens = voxels.reshape(-1, model_width)
    normed = layer_norm(flat_tokens, norm_gain)
    qkv = jnp.dot(normed, qkv_weight, preferred_element_type=jnp.float32).astype(jnp.bfloat16)
    queries = qkv[:, :model_width].reshape(-1, block_size, HEADS, HEAD_DIM)
    key_table = qkv[:, model_width:2 * model_width].reshape(-1, block_size, HEADS, HEAD_DIM)
    value_table = qkv[:, 2 * model_width:].reshape(-1, block_size, HEADS, HEAD_DIM)
    block_count = queries.shape[0]
    block_ids = jnp.arange(block_count, dtype=jnp.int32)
    key_lists = jnp.concatenate([block_ids[:, None], neighbours.reshape(block_count, NBR).astype(jnp.int32)], axis=1)
    score_scale = HEAD_DIM ** (-0.5)

    def attend(operands):
        query_block, key_list = operands
        present = key_list >= 0
        clamped = jnp.where(present, key_list, 0).astype(jnp.int32)
        key_rows = key_table[clamped].reshape(-1, HEADS, HEAD_DIM).astype(jnp.float32)
        value_rows = value_table[clamped].reshape(-1, HEADS, HEAD_DIM).astype(jnp.float32)
        scores = jnp.einsum('shd,khd->hsk', query_block.astype(jnp.float32), key_rows) * score_scale
        key_mask = jnp.repeat(present, block_size)
        scores = jnp.where(key_mask[None, None, :], scores, -1e+30)
        attn_probs = jax.nn.softmax(scores, axis=-1).astype(jnp.bfloat16)
        attended = jnp.einsum('hsk,khd->shd', attn_probs.astype(jnp.float32), value_rows)
        return attended.reshape(block_size, model_width).astype(jnp.bfloat16)
    mixed = lax.map(attend, (queries, key_lists))
    projected = jnp.dot(mixed.reshape(-1, model_width), out_weight, preferred_element_type=jnp.float32)
    result = flat_tokens.astype(jnp.float32) + projected
    return result.astype(jnp.bfloat16).reshape(voxels.shape)
```

```python
import functools

import jax
import jax.numpy as jnp
from jax import lax
from jax.experimental import pallas as pl
from jax.experimental.pallas import tpu as pltpu
from jax.sharding import PartitionSpec as P

HEAD_DIM = 64
MESH = pl.DeviceIdType.MESH
SIB, UP, DOWN, ACROSS, REGION = range(5)


def padded(value, sides, width):
    for axis, dim in sides:
        devices, length = (lax.axis_size(axis), value.shape[dim])
        up = [(i, (i + 1) % devices) for i in range(devices - 1)]
        down = [(j, i) for i, j in up]
        last = lax.slice_in_dim(value, length - width, length, axis=dim)
        first = lax.slice_in_dim(value, 0, width, axis=dim)
        before = lax.ppermute(last, axis, up)
        after = lax.ppermute(first, axis, down)
        value = jnp.concatenate([before, value, after], axis=dim)
    return value


def exchange_kernel(owners, x_ref, wq_ref, wo_ref, xs_ref, gq_ref, go_ref,
                    send_q, recv_q, send_o, recv_o, send_x, recv_x, local_sem):
    planes = owners // 4
    region = lax.axis_index("region")
    owner = lax.axis_index("owner")
    core = lax.rem(owner, 2)
    row = lax.rem(owner // 2, 2)
    plane = owner // 4
    side_owner = owner + 2 * core - 1
    has_side = jnp.logical_and(side_owner >= 0, side_owner < owners)
    has_up = plane < planes - 1
    has_down = plane > 0

    def owner_of(z, y, c):
        return z * 4 + y * 2 + c

    targets = {
        SIB: (region, owner_of(plane, row, 1 - core)),
        UP: (region, owner_of(plane + 1, row, core)),
        DOWN: (region, owner_of(plane - 1, row, core)),
        ACROSS: (region, owner_of(plane, 1 - row, core)),
        REGION: (1 - region, owner),
    }
    conditions = {SIB: None, UP: has_up, DOWN: has_down, ACROSS: None, REGION: None}
    side = (region, side_owner)

    barrier = pltpu.get_barrier_semaphore()
    for kind, target in targets.items():
        def greet(target=target):
            pl.semaphore_signal(barrier, inc=1, device_id=target, device_id_type=MESH)
        if conditions[kind] is None:
            greet()
        else:
            pl.when(conditions[kind])(greet)

    @pl.when(has_side)
    def _():
        pl.semaphore_signal(barrier, inc=1, device_id=side, device_id_type=MESH)

    pl.semaphore_wait(
        barrier,
        3 + has_up.astype(jnp.int32) + has_down.astype(jnp.int32) + has_side.astype(jnp.int32),
    )

    pending = []

    def run(cond, fn):
        if cond is None:
            fn()
        else:
            pl.when(cond)(fn)

    def both(a, b):
        if a is None:
            return b
        return a if b is None else jnp.logical_and(a, b)

    def start(cond, make):
        run(cond, lambda: make().start())
        pending.append((cond, lambda: make().wait_send()))

    weights = {
        "q": (wq_ref, gq_ref, send_q, recv_q),
        "o": (wo_ref, go_ref, send_o, recv_o),
    }

    def rows_of(ref, shard, src):
        depth = shard.shape[0]
        return ref.at[pl.ds(pl.multiple_of(src * depth, depth), depth), :]

    def send(name, kind, src, cond, own=False):
        shard, full, send_sem, recv_sem = weights[name]
        cond = both(cond, conditions[kind])

        def make():
            return pltpu.make_async_remote_copy(
                src_ref=shard if own else rows_of(full, shard, src),
                dst_ref=rows_of(full, shard, src),
                send_sem=send_sem.at[kind, src],
                recv_sem=recv_sem.at[src],
                device_id=targets[kind],
                device_id_type=MESH,
            )

        start(cond, make)

    def arrive(name, src, cond):
        shard, full, send_sem, recv_sem = weights[name]

        def wait():
            pltpu.make_async_remote_copy(
                src_ref=rows_of(full, shard, src),
                dst_ref=rows_of(full, shard, src),
                send_sem=send_sem.at[SIB, src],
                recv_sem=recv_sem.at[src],
                device_id=targets[SIB],
                device_id_type=MESH,
            ).wait_recv()

        run(cond, wait)

    def send_block(src_ref, slot, target, sem, cond):
        def make():
            return pltpu.make_async_remote_copy(
                src_ref=src_ref,
                dst_ref=xs_ref.at[slot],
                send_sem=send_x.at[sem],
                recv_sem=recv_x.at[slot],
                device_id=target,
                device_id_type=MESH,
            )

        start(cond, make)

    def arrive_block(slot, cond):
        def wait():
            pltpu.make_async_remote_copy(
                src_ref=xs_ref.at[slot],
                dst_ref=xs_ref.at[slot],
                send_sem=send_x.at[0],
                recv_sem=recv_x.at[slot],
                device_id=targets[SIB],
                device_id_type=MESH,
            ).wait_recv()

        run(cond, wait)

    def ident(r, z, y, c):
        return r * owners + owner_of(z, y, c)

    me = ident(region, plane, row, core)
    for kind in (UP, DOWN, ACROSS):
        send("q", kind, me, None, own=True)
    send_block(x_ref, 4, targets[REGION], 0, None)
    send("q", REGION, me, None, own=True)
    send("o", ACROSS, me, None, own=True)
    send_block(x_ref, 1 - core, side, 1, has_side)
    send("q", SIB, me, None, own=True)
    send("o", SIB, me, None, own=True)
    send_block(x_ref, core, targets[SIB], 2, None)
    local_q = pltpu.make_async_copy(wq_ref, rows_of(gq_ref, wq_ref, me), local_sem.at[0])
    local_o = pltpu.make_async_copy(wo_ref, rows_of(go_ref, wo_ref, me), local_sem.at[1])
    local_q.start()
    local_o.start()

    def at_distance(d):
        if d == 0:
            return [(plane, None, ())]
        return [
            (plane - d, plane - d >= 0, (UP,)),
            (plane + d, plane + d < planes, (DOWN,)),
        ]

    def row_step(d):
        for z, cond, _ in at_distance(d):
            src = ident(region, z, 1 - row, core)
            arrive("q", src, cond)
            send("q", REGION, src, cond)
            send("q", SIB, src, cond)

    def plane_step(d):
        for z, cond, onward in at_distance(d):
            src = ident(region, z, row, core)
            arrive("q", src, cond)
            for kind in onward + (ACROSS, REGION, SIB):
                send("q", kind, src, cond)

    row_step(0)
    for d in range(1, planes):
        plane_step(d)
        row_step(d)
        if d == 1:
            arrive_block(4, None)
            send_block(xs_ref.at[4], 2 + core, targets[SIB], 3, None)
            send_block(xs_ref.at[4], 3 - core, side, 4, has_side)

    send("o", REGION, me, None, own=True)
    for kind in (UP, DOWN):
        send("o", kind, me, None, own=True)
    src = ident(region, plane, 1 - row, core)
    arrive("o", src, None)
    for kind in (REGION, UP, DOWN, SIB):
        send("o", kind, src, None)
    for y in (row, 1 - row):
        src = ident(1 - region, plane, y, core)
        arrive("o", src, None)
        for kind in (UP, DOWN, SIB):
            send("o", kind, src, None)
    def region_q(d):
        order = [row, 1 - row] if d == 0 else [row, 1 - row]
        for y in order:
            for z, cond, _ in at_distance(d):
                src = ident(1 - region, z, y, core)
                arrive("q", src, cond)
                send("q", SIB, src, cond)

    def plane_o(d):
        for r, y in ((region, row), (region, 1 - row), (1 - region, row), (1 - region, 1 - row)):
            for z, cond, onward in at_distance(d):
                src = ident(r, z, y, core)
                arrive("o", src, cond)
                for kind in onward + (SIB,):
                    send("o", kind, src, cond)

    region_q(0)
    for d in range(1, planes):
        region_q(d)
        plane_o(d)

    for name in ("q", "o"):
        for d in range(planes):
            for r in (region, 1 - region):
                for y in (row, 1 - row):
                    for z, cond, _ in at_distance(d):
                        arrive(name, ident(r, z, y, 1 - core), cond)
    arrive_block(1 - core, None)
    arrive_block(3 - core, None)
    arrive_block(core, has_side)
    arrive_block(2 + core, has_side)
    for cond, wait in pending:
        run(cond, wait)
    local_q.wait()
    local_o.wait()


def exchange(block, qkv_weight, out_weight):
    owners = lax.axis_size("owner")
    devices = lax.axis_size("region") * owners
    anywhere = pl.BlockSpec(memory_space=pl.ANY)
    return pl.pallas_call(
        functools.partial(exchange_kernel, owners),
        out_shape=[
            jax.ShapeDtypeStruct((5,) + block.shape, block.dtype),
            jax.ShapeDtypeStruct((devices * qkv_weight.shape[0], qkv_weight.shape[1]), qkv_weight.dtype),
            jax.ShapeDtypeStruct((devices * out_weight.shape[0], out_weight.shape[1]), out_weight.dtype),
        ],
        in_specs=[anywhere] * 3,
        out_specs=[anywhere] * 3,
        scratch_shapes=[
            pltpu.SemaphoreType.DMA((5, devices)),
            pltpu.SemaphoreType.DMA((devices,)),
            pltpu.SemaphoreType.DMA((5, devices)),
            pltpu.SemaphoreType.DMA((devices,)),
            pltpu.SemaphoreType.DMA((5,)),
            pltpu.SemaphoreType.DMA((5,)),
            pltpu.SemaphoreType.DMA((2,)),
        ],
        compiler_params=pltpu.CompilerParams(collective_id=0, has_side_effects=True),
        name="exchange",
    )(block, qkv_weight, out_weight)


def layer_norm(inputs, norm_gain):
    widened = inputs.astype(jnp.float32)
    average = jnp.mean(widened, axis=-1, keepdims=True)
    spread = jnp.mean((widened - average) ** 2, axis=-1, keepdims=True)
    return ((widened - average) * lax.rsqrt(spread + 1e-06) * norm_gain).astype(jnp.bfloat16)


def attend_kernel(listed_ref, x_ref, xs_ref, gain_ref, bias_ref, wq_ref, wo_ref, out_ref,
                  normed_ref, q_ref, kv_ref, mixed_ref):
    tokens, width = x_ref.shape
    others = xs_ref.shape[0]
    gain = gain_ref[...]
    normed_ref[0:tokens, :] = layer_norm(x_ref[...], gain)

    @pl.loop(0, others)
    def _(slot):
        rows = pl.ds(pl.multiple_of((slot + 1) * tokens, tokens), tokens)
        block = xs_ref[slot].astype(jnp.float32)
        block = jnp.where(listed_ref[slot] > 0, block, 0.0)
        normed_ref[rows, :] = layer_norm(block, gain)

    tile = min(512, width)

    @pl.loop(0, width // tile)
    def _(step):
        cols = pl.ds(pl.multiple_of(step * tile, tile), tile)
        part = jnp.dot(normed_ref[0:tokens, :], wq_ref[:, cols], preferred_element_type=jnp.float32)
        q_ref[:, cols] = part.astype(jnp.bfloat16) * jnp.bfloat16(HEAD_DIM ** (-0.5))

    @pl.loop(0, 2 * width // tile)
    def _(step):
        cols = pl.ds(pl.multiple_of(step * tile, tile), tile)
        from_cols = pl.ds(pl.multiple_of(width + step * tile, tile), tile)
        kv_ref[:, cols] = jnp.dot(
            normed_ref[...], wq_ref[:, from_cols], preferred_element_type=jnp.float32
        ).astype(jnp.bfloat16)

    pair = 2 * HEAD_DIM
    low = lax.broadcasted_iota(jnp.int32, (tokens, pair), 1) < HEAD_DIM
    bias = bias_ref[...]

    @pl.loop(0, width // pair)
    def _(group):
        cols = pl.ds(pl.multiple_of(group * pair, pair), pair)
        value_cols = pl.ds(pl.multiple_of(width + group * pair, pair), pair)
        queries = q_ref[:, cols]
        keys = kv_ref[:, cols]
        values = kv_ref[:, value_cols]
        halves = []
        for mine in (low, jnp.logical_not(low)):
            query = jnp.where(mine, queries, jnp.zeros_like(queries))
            scores = lax.dot_general(
                query, keys, (((1,), (1,)), ((), ())), preferred_element_type=jnp.float32
            ) + bias
            shifted = jnp.exp(scores - jnp.max(scores, axis=-1, keepdims=True))
            total = jnp.sum(shifted, axis=-1, keepdims=True)
            mixed = jnp.dot(shifted.astype(jnp.bfloat16), values, preferred_element_type=jnp.float32)
            halves.append(mixed / total)
        mixed_ref[:, cols] = jnp.where(low, halves[0], halves[1]).astype(jnp.bfloat16)

    @pl.loop(0, width // tile)
    def _(step):
        cols = pl.ds(pl.multiple_of(step * tile, tile), tile)
        projected = jnp.dot(mixed_ref[...], wo_ref[:, cols], preferred_element_type=jnp.float32)
        out_ref[:, cols] = (x_ref[:, cols].astype(jnp.float32) + projected).astype(out_ref.dtype)


def attend(listed, block, others, norm_gain, bias, qkv_weight, out_weight):
    tokens, width = block.shape
    count = (others.shape[0] + 1) * tokens
    vmem = pl.BlockSpec(memory_space=pltpu.VMEM)
    return pl.pallas_call(
        attend_kernel,
        out_shape=jax.ShapeDtypeStruct(block.shape, block.dtype),
        in_specs=[pl.BlockSpec(memory_space=pltpu.SMEM)] + [vmem] * 6,
        out_specs=vmem,
        scratch_shapes=[
            pltpu.VMEM((count, width), jnp.bfloat16),
            pltpu.VMEM((tokens, width), jnp.bfloat16),
            pltpu.VMEM((count, 2 * width), jnp.bfloat16),
            pltpu.VMEM((tokens, width), jnp.bfloat16),
        ],
        compiler_params=pltpu.CompilerParams(vmem_limit_bytes=60 * 1024 * 1024),
        name="attend",
    )(listed, block, others, norm_gain, bias, qkv_weight, out_weight)


def shards(voxels, norm_gain, qkv_weight, out_weight, neighbours):
    block_size, model_width = voxels.shape[-2:]
    block = voxels.reshape(block_size, model_width)
    regions, owners = (lax.axis_size("region"), lax.axis_size("owner"))
    region, owner = (lax.axis_index("region"), lax.axis_index("owner"))
    if regions == 2 and owners % 4 == 0 and owners > 4:
        others, full_qkv, full_out = exchange(block, qkv_weight, out_weight)
        offsets = [(0, -1), (0, 1), (1 - 2 * region, -1), (1 - 2 * region, 1), (1 - 2 * region, 0)]
    else:
        wide = padded(voxels[:, :, 0], (("owner", 1), ("region", 0)), 1)
        wide = wide.reshape(-1, block_size, model_width)
        middle = wide.shape[0] // 2
        others = jnp.concatenate([wide[:middle], wide[middle + 1:]], axis=0)
        full_qkv = lax.all_gather(qkv_weight, ("region", "owner"), axis=0, tiled=True)
        full_out = lax.all_gather(out_weight, ("region", "owner"), axis=0, tiled=True)
        offsets = [(i, j) for i in (-1, 0, 1) for j in (-1, 0, 1) if i or j]
    numbers = []
    for up, along in offsets:
        inside = (owner + along >= 0) & (owner + along < owners)
        number = (region + up) * owners + owner + along
        numbers.append(jnp.where(inside & (number >= 0), number, -2))
    listed = jnp.any(neighbours.reshape(1, -1) == jnp.stack(numbers)[:, None], axis=1)
    present = jnp.concatenate([jnp.ones((1,), bool), listed])
    bias = jnp.repeat(jnp.where(present, 0.0, -1e30).astype(jnp.float32), block_size)[None, :]
    out = attend(
        listed.astype(jnp.int32), block, others, norm_gain[None, :], bias, full_qkv, full_out
    )
    return out.reshape(voxels.shape)


def solution(mesh):
    return jax.shard_map(
        shards,
        mesh=mesh,
        in_specs=(
            P("region", "owner", None, None, None),
            P(),
            P(("region", "owner"), None),
            P(("region", "owner"), None),
            P("region", "owner", None, None),
        ),
        out_specs=P("region", "owner", None, None, None),
        check_vma=False,
    )
```

```python
import functools

import jax
import jax.numpy as jnp
from jax import lax
from jax.experimental import pallas as pl
from jax.experimental.pallas import tpu as pltpu
from jax.sharding import PartitionSpec as P

HEAD_DIM = 64
MESH = pl.DeviceIdType.MESH
GROUPS = 4
SIB, UP, DOWN, ACROSS, REGION = range(5)


def padded(value, sides, width):
    for axis, dim in sides:
        devices, length = (lax.axis_size(axis), value.shape[dim])
        up = [(i, (i + 1) % devices) for i in range(devices - 1)]
        down = [(j, i) for i, j in up]
        last = lax.slice_in_dim(value, length - width, length, axis=dim)
        first = lax.slice_in_dim(value, 0, width, axis=dim)
        before = lax.ppermute(last, axis, up)
        after = lax.ppermute(first, axis, down)
        value = jnp.concatenate([before, value, after], axis=dim)
    return value


def layer_norm(inputs, norm_gain):
    widened = inputs.astype(jnp.float32)
    average = jnp.mean(widened, axis=-1, keepdims=True)
    spread = jnp.mean((widened - average) ** 2, axis=-1, keepdims=True)
    return ((widened - average) * lax.rsqrt(spread + 1e-06) * norm_gain).astype(jnp.bfloat16)


def attend_heads(queries, keys, values, bias):
    tokens, pair = queries.shape
    low = lax.broadcasted_iota(jnp.int32, (tokens, pair), 1) < HEAD_DIM
    halves = []
    for mine in (low, jnp.logical_not(low)):
        query = jnp.where(mine, queries, jnp.zeros_like(queries))
        scores = lax.dot_general(
            query, keys, (((1,), (1,)), ((), ())), preferred_element_type=jnp.float32
        ) + bias
        shifted = jnp.exp(scores - jnp.max(scores, axis=-1, keepdims=True))
        total = jnp.sum(shifted, axis=-1, keepdims=True)
        mixed = jnp.dot(shifted.astype(jnp.bfloat16), values, preferred_element_type=jnp.float32)
        halves.append(mixed / total)
    return jnp.where(low, halves[0], halves[1]).astype(jnp.bfloat16)


def fused_kernel(owners, x_ref, wq_ref, wo_ref, gain_ref, bias_ref, out_ref,
                 xs_ref, gq_ref, go_ref, normed_ref, q_ref, kv_ref, mixed_ref,
                 send_q, recv_q, send_o, recv_o, send_x, recv_x, local_sem):
    groups = wq_ref.shape[0]
    share = wq_ref.shape[2] // 3
    tokens, width = x_ref.shape
    others = xs_ref.shape[0]
    planes = owners // 4
    region = lax.axis_index("region")
    owner = lax.axis_index("owner")
    core = lax.rem(owner, 2)
    row = lax.rem(owner // 2, 2)
    plane = owner // 4
    side_owner = owner + 2 * core - 1
    has_side = jnp.logical_and(side_owner >= 0, side_owner < owners)
    has_up = plane < planes - 1
    has_down = plane > 0

    def owner_of(z, y, c):
        return z * 4 + y * 2 + c

    def ident(r, z, y, c):
        return r * owners + owner_of(z, y, c)

    targets = {
        SIB: (region, owner_of(plane, row, 1 - core)),
        UP: (region, owner_of(plane + 1, row, core)),
        DOWN: (region, owner_of(plane - 1, row, core)),
        ACROSS: (region, owner_of(plane, 1 - row, core)),
        REGION: (1 - region, owner),
    }
    conditions = {SIB: None, UP: has_up, DOWN: has_down, ACROSS: None, REGION: None}
    side = (region, side_owner)

    def run(cond, fn):
        if cond is None:
            fn()
        else:
            pl.when(cond)(fn)

    def both(a, b):
        if a is None:
            return b
        return a if b is None else jnp.logical_and(a, b)

    barrier = pltpu.get_barrier_semaphore()

    def greet(target):
        pl.semaphore_signal(barrier, inc=1, device_id=target, device_id_type=MESH)

    for kind, target in targets.items():
        run(conditions[kind], functools.partial(greet, target))
    run(has_side, functools.partial(greet, side))
    pl.semaphore_wait(
        barrier,
        3 + has_up.astype(jnp.int32) + has_down.astype(jnp.int32) + has_side.astype(jnp.int32),
    )

    pending = []

    def start(cond, make):
        run(cond, lambda: make().start())
        pending.append((cond, lambda: make().wait_send()))

    def whole(name):
        return go_ref if name == "o" else gq_ref.at[name]

    def own_shard(name):
        return wo_ref if name == "o" else wq_ref.at[name]

    def rows_of(name, src):
        depth = wo_ref.shape[0]
        return whole(name).at[pl.ds(pl.multiple_of(src * depth, depth), depth), :]

    def send_sem(name, kind, src):
        return send_o.at[kind, src // 2] if name == "o" else send_q.at[name, kind, src // 2]

    def recv_sem(name, src):
        return recv_o.at[src] if name == "o" else recv_q.at[name, src]

    def send(name, kind, src, cond, own=False):
        def make():
            return pltpu.make_async_remote_copy(
                src_ref=own_shard(name) if own else rows_of(name, src),
                dst_ref=rows_of(name, src),
                send_sem=send_sem(name, kind, src),
                recv_sem=recv_sem(name, src),
                device_id=targets[kind],
                device_id_type=MESH,
            )

        start(both(cond, conditions[kind]), make)

    def arrive(name, src, cond):
        def wait():
            pltpu.make_async_remote_copy(
                src_ref=rows_of(name, src),
                dst_ref=rows_of(name, src),
                send_sem=send_sem(name, SIB, src),
                recv_sem=recv_sem(name, src),
                device_id=targets[SIB],
                device_id_type=MESH,
            ).wait_recv()

        run(cond, wait)

    def block_copy(src_ref, slot, target, sem):
        return pltpu.make_async_remote_copy(
            src_ref=src_ref,
            dst_ref=xs_ref.at[slot],
            send_sem=send_x.at[sem],
            recv_sem=recv_x.at[slot],
            device_id=target,
            device_id_type=MESH,
        )

    def send_block(src_ref, slot, target, sem, cond):
        start(cond, lambda: block_copy(src_ref, slot, target, sem))

    def arrive_block(slot, cond):
        run(cond, lambda: block_copy(xs_ref.at[slot], slot, targets[SIB], 0).wait_recv())

    me = ident(region, plane, row, core)

    def at_distance(d):
        if d == 0:
            return [(plane, None, ())]
        return [
            (plane - d, plane - d >= 0, (UP,)),
            (plane + d, plane + d < planes, (DOWN,)),
        ]

    def row_step(g, d):
        for z, cond, _ in at_distance(d):
            src = ident(region, z, 1 - row, core)
            arrive(g, src, cond)
            send(g, REGION, src, cond)
            send(g, SIB, src, cond)

    def plane_step(g, d):
        for z, cond, onward in at_distance(d):
            src = ident(region, z, row, core)
            arrive(g, src, cond)
            for kind in onward + (ACROSS, REGION, SIB):
                send(g, kind, src, cond)

    def own_step(g):
        for kind in (UP, DOWN, ACROSS, REGION, SIB):
            send(g, kind, me, None, own=True)

    def region_step(g, d):
        for y in (row, 1 - row):
            for z, cond, _ in at_distance(d):
                src = ident(1 - region, z, y, core)
                arrive(g, src, cond)
                send(g, SIB, src, cond)

    def sibling_step(name):
        for d in range(planes):
            for r in (region, 1 - region):
                for y in (row, 1 - row):
                    for z, cond, _ in at_distance(d):
                        arrive(name, ident(r, z, y, 1 - core), cond)

    def near_steps(g, own=True):
        steps = [functools.partial(own_step, g)] if own else []
        steps.append(functools.partial(row_step, g, 0))
        for d in range(1, planes):
            steps.append(functools.partial(plane_step, g, d))
            steps.append(functools.partial(row_step, g, d))
        return steps

    def far_steps(g):
        steps = [functools.partial(region_step, g, d) for d in range(planes)]
        return steps + [functools.partial(sibling_step, g)]

    def out_across():
        src = ident(region, plane, 1 - row, core)
        arrive("o", src, None)
        for kind in (REGION, UP, DOWN, SIB):
            send("o", kind, src, None)

    def out_region():
        for y in (row, 1 - row):
            src = ident(1 - region, plane, y, core)
            arrive("o", src, None)
            for kind in (UP, DOWN, SIB):
                send("o", kind, src, None)

    def out_plane(d):
        for r, y in ((region, row), (region, 1 - row), (1 - region, row), (1 - region, 1 - row)):
            for z, cond, onward in at_distance(d):
                src = ident(r, z, y, core)
                arrive("o", src, cond)
                for kind in onward + (SIB,):
                    send("o", kind, src, cond)

    def out_own():
        for kind in (ACROSS, REGION, UP, DOWN, SIB):
            send("o", kind, me, None, own=True)

    gain = gain_ref[...]

    def norm_block(slot):
        rows = pl.ds(pl.multiple_of((slot + 1) * tokens, tokens), tokens)
        normed_ref[rows, :] = layer_norm(xs_ref[slot], gain)

    bias = bias_ref[...]
    pair = 2 * HEAD_DIM

    def project(g, first, rows):
        kv_ref[first:first + rows, :] = jnp.dot(
            normed_ref[first:first + rows, :], gq_ref[g, :, share:],
            preferred_element_type=jnp.float32,
        ).astype(jnp.bfloat16)

    def project_queries(g):
        part = jnp.dot(
            normed_ref[0:tokens, :], gq_ref[g, :, 0:share], preferred_element_type=jnp.float32
        )
        q_ref[...] = part.astype(jnp.bfloat16) * jnp.bfloat16(HEAD_DIM ** (-0.5))

    def attend_pair(g, at):
        mixed_ref[:, g * share + at:g * share + at + pair] = attend_heads(
            q_ref[:, at:at + pair],
            kv_ref[:, at:at + pair],
            kv_ref[:, share + at:share + at + pair],
            bias,
        )

    def compute_steps(g):
        count = (others + 1) * tokens
        steps = [functools.partial(project_queries, g)]
        steps += [functools.partial(project, g, i, tokens) for i in range(0, count, tokens)]
        return steps + [functools.partial(attend_pair, g, at) for at in range(0, share, pair)]

    def interleave(work, steps):
        done = 0
        for i, piece in enumerate(work):
            piece()
            due = (i + 1) * len(steps) // len(work)
            for step in steps[done:due]:
                step()
            done = due

    for kind in (UP, DOWN, ACROSS):
        send(0, kind, me, None, own=True)
    send_block(x_ref, 4, targets[REGION], 0, None)
    for kind in (REGION, SIB):
        send(0, kind, me, None, own=True)
    send_block(x_ref, 1 - core, side, 1, has_side)
    send_block(x_ref, core, targets[SIB], 2, None)
    local = [
        pltpu.make_async_copy(own_shard(name), rows_of(name, me), local_sem.at[i])
        for i, name in enumerate(list(range(groups)) + ["o"])
    ]
    for copy in local:
        copy.start()

    @pl.when(jnp.logical_not(has_side))
    def _():
        xs_ref[core] = jnp.zeros((tokens, width), xs_ref.dtype)
        xs_ref[2 + core] = jnp.zeros((tokens, width), xs_ref.dtype)

    normed_ref[0:tokens, :] = layer_norm(x_ref[...], gain)

    def relay():
        arrive_block(4, None)
        send_block(xs_ref.at[4], 2 + core, targets[SIB], 3, None)
        send_block(xs_ref.at[4], 3 - core, side, 4, has_side)

    def norm_step(slot, cond, wait=True):
        if wait:
            arrive_block(slot, cond)
        norm_block(slot)

    first = near_steps(0, own=False)
    for step in first[:3] + [relay] + first[3:]:
        step()
    norms = [
        functools.partial(norm_step, 1 - core, None),
        functools.partial(norm_step, 4, None, False),
        functools.partial(norm_step, core, has_side),
        functools.partial(norm_step, 3 - core, None),
        functools.partial(norm_step, 2 + core, has_side),
    ]
    interleave(norms, near_steps(1))
    for copy in local:
        copy.wait()
    for step in far_steps(0):
        step()
    out_steps = [out_own, out_across, out_region] + [
        functools.partial(out_plane, d) for d in range(1, planes)
    ] + [functools.partial(sibling_step, "o")]
    half = len(out_steps) // 2
    for g in range(groups):
        steps = []
        if g + 2 < groups:
            steps += near_steps(g + 2)
        if g + 2 == groups:
            steps += out_steps[:half]
        if g + 1 < groups:
            steps += far_steps(g + 1)
        if g + 1 == groups:
            steps += out_steps[half:]
        interleave(compute_steps(g), steps)

    tile = min(512, width)
    for at in range(0, width, tile):
        projected = jnp.dot(
            mixed_ref[...], go_ref[:, at:at + tile], preferred_element_type=jnp.float32
        )
        out_ref[:, at:at + tile] = (
            x_ref[:, at:at + tile].astype(jnp.float32) + projected
        ).astype(out_ref.dtype)
    for cond, wait in pending:
        run(cond, wait)


def fused(block, qkv_weight, out_weight, norm_gain, bias):
    owners = lax.axis_size("owner")
    devices = lax.axis_size("region") * owners
    tokens, width = block.shape
    depth = qkv_weight.shape[0]
    groups = GROUPS
    share = width // groups
    parted = qkv_weight.reshape(depth, 3, groups, share).transpose(2, 0, 1, 3)
    parted = parted.reshape(groups, depth, 3 * share)
    count = bias.shape[1]
    vmem = pl.BlockSpec(memory_space=pltpu.VMEM)
    return pl.pallas_call(
        functools.partial(fused_kernel, owners),
        out_shape=jax.ShapeDtypeStruct(block.shape, block.dtype),
        in_specs=[vmem] * 5,
        out_specs=vmem,
        scratch_shapes=[
            pltpu.VMEM((5, tokens, width), block.dtype),
            pltpu.VMEM((groups, devices * depth, 3 * share), qkv_weight.dtype),
            pltpu.VMEM((devices * depth, width), out_weight.dtype),
            pltpu.VMEM((count, width), jnp.bfloat16),
            pltpu.VMEM((tokens, share), jnp.bfloat16),
            pltpu.VMEM((count, 2 * share), jnp.bfloat16),
            pltpu.VMEM((tokens, width), jnp.bfloat16),
            pltpu.SemaphoreType.DMA((groups, 5, devices // 2)),
            pltpu.SemaphoreType.DMA((groups, devices)),
            pltpu.SemaphoreType.DMA((5, devices // 2)),
            pltpu.SemaphoreType.DMA((devices,)),
            pltpu.SemaphoreType.DMA((5,)),
            pltpu.SemaphoreType.DMA((5,)),
            pltpu.SemaphoreType.DMA((groups + 1,)),
        ],
        compiler_params=pltpu.CompilerParams(
            collective_id=0, has_side_effects=True, vmem_limit_bytes=60 * 1024 * 1024
        ),
        name="fused",
    )(block, parted, out_weight, norm_gain, bias)


def attend_kernel(listed_ref, x_ref, xs_ref, gain_ref, bias_ref, wq_ref, wo_ref, out_ref,
                  normed_ref, q_ref, kv_ref, mixed_ref):
    tokens, width = x_ref.shape
    others = xs_ref.shape[0]
    gain = gain_ref[...]
    normed_ref[0:tokens, :] = layer_norm(x_ref[...], gain)

    @pl.loop(0, others)
    def _(slot):
        rows = pl.ds(pl.multiple_of((slot + 1) * tokens, tokens), tokens)
        block = xs_ref[slot].astype(jnp.float32)
        block = jnp.where(listed_ref[slot] > 0, block, 0.0)
        normed_ref[rows, :] = layer_norm(block, gain)

    tile = min(512, width)

    @pl.loop(0, width // tile)
    def _(step):
        cols = pl.ds(pl.multiple_of(step * tile, tile), tile)
        part = jnp.dot(normed_ref[0:tokens, :], wq_ref[:, cols], preferred_element_type=jnp.float32)
        q_ref[:, cols] = part.astype(jnp.bfloat16) * jnp.bfloat16(HEAD_DIM ** (-0.5))

    @pl.loop(0, 2 * width // tile)
    def _(step):
        cols = pl.ds(pl.multiple_of(step * tile, tile), tile)
        from_cols = pl.ds(pl.multiple_of(width + step * tile, tile), tile)
        kv_ref[:, cols] = jnp.dot(
            normed_ref[...], wq_ref[:, from_cols], preferred_element_type=jnp.float32
        ).astype(jnp.bfloat16)

    pair = 2 * HEAD_DIM
    low = lax.broadcasted_iota(jnp.int32, (tokens, pair), 1) < HEAD_DIM
    bias = bias_ref[...]

    @pl.loop(0, width // pair)
    def _(group):
        cols = pl.ds(pl.multiple_of(group * pair, pair), pair)
        value_cols = pl.ds(pl.multiple_of(width + group * pair, pair), pair)
        queries = q_ref[:, cols]
        keys = kv_ref[:, cols]
        values = kv_ref[:, value_cols]
        halves = []
        for mine in (low, jnp.logical_not(low)):
            query = jnp.where(mine, queries, jnp.zeros_like(queries))
            scores = lax.dot_general(
                query, keys, (((1,), (1,)), ((), ())), preferred_element_type=jnp.float32
            ) + bias
            shifted = jnp.exp(scores - jnp.max(scores, axis=-1, keepdims=True))
            total = jnp.sum(shifted, axis=-1, keepdims=True)
            mixed = jnp.dot(shifted.astype(jnp.bfloat16), values, preferred_element_type=jnp.float32)
            halves.append(mixed / total)
        mixed_ref[:, cols] = jnp.where(low, halves[0], halves[1]).astype(jnp.bfloat16)

    @pl.loop(0, width // tile)
    def _(step):
        cols = pl.ds(pl.multiple_of(step * tile, tile), tile)
        projected = jnp.dot(mixed_ref[...], wo_ref[:, cols], preferred_element_type=jnp.float32)
        out_ref[:, cols] = (x_ref[:, cols].astype(jnp.float32) + projected).astype(out_ref.dtype)


def attend(listed, block, others, norm_gain, bias, qkv_weight, out_weight):
    tokens, width = block.shape
    count = (others.shape[0] + 1) * tokens
    vmem = pl.BlockSpec(memory_space=pltpu.VMEM)
    return pl.pallas_call(
        attend_kernel,
        out_shape=jax.ShapeDtypeStruct(block.shape, block.dtype),
        in_specs=[pl.BlockSpec(memory_space=pltpu.SMEM)] + [vmem] * 6,
        out_specs=vmem,
        scratch_shapes=[
            pltpu.VMEM((count, width), jnp.bfloat16),
            pltpu.VMEM((tokens, width), jnp.bfloat16),
            pltpu.VMEM((count, 2 * width), jnp.bfloat16),
            pltpu.VMEM((tokens, width), jnp.bfloat16),
        ],
        compiler_params=pltpu.CompilerParams(vmem_limit_bytes=60 * 1024 * 1024),
        name="attend",
    )(listed, block, others, norm_gain, bias, qkv_weight, out_weight)


def shards(voxels, norm_gain, qkv_weight, out_weight, neighbours):
    block_size, model_width = voxels.shape[-2:]
    block = voxels.reshape(block_size, model_width)
    regions, owners = (lax.axis_size("region"), lax.axis_size("owner"))
    region, owner = (lax.axis_index("region"), lax.axis_index("owner"))
    together = regions == 2 and owners % 4 == 0 and owners > 4
    if together:
        offsets = [(0, -1), (0, 1), (1 - 2 * region, -1), (1 - 2 * region, 1), (1 - 2 * region, 0)]
    else:
        wide = padded(voxels[:, :, 0], (("owner", 1), ("region", 0)), 1)
        wide = wide.reshape(-1, block_size, model_width)
        middle = wide.shape[0] // 2
        others = jnp.concatenate([wide[:middle], wide[middle + 1:]], axis=0)
        full_qkv = lax.all_gather(qkv_weight, ("region", "owner"), axis=0, tiled=True)
        full_out = lax.all_gather(out_weight, ("region", "owner"), axis=0, tiled=True)
        offsets = [(i, j) for i in (-1, 0, 1) for j in (-1, 0, 1) if i or j]
    numbers = []
    for up, along in offsets:
        inside = (owner + along >= 0) & (owner + along < owners)
        number = (region + up) * owners + owner + along
        numbers.append(jnp.where(inside & (number >= 0), number, -2))
    listed = jnp.any(neighbours.reshape(1, -1) == jnp.stack(numbers)[:, None], axis=1)
    present = jnp.concatenate([jnp.ones((1,), bool), listed])
    bias = jnp.repeat(jnp.where(present, 0.0, -1e30).astype(jnp.float32), block_size)[None, :]
    if together:
        out = fused(block, qkv_weight, out_weight, norm_gain[None, :], bias)
        return out.reshape(voxels.shape)
    out = attend(
        listed.astype(jnp.int32), block, others, norm_gain[None, :], bias, full_qkv, full_out
    )
    return out.reshape(voxels.shape)


def solution(mesh):
    return jax.shard_map(
        shards,
        mesh=mesh,
        in_specs=(
            P("region", "owner", None, None, None),
            P(),
            P(("region", "owner"), None),
            P(("region", "owner"), None),
            P("region", "owner", None, None),
        ),
        out_specs=P("region", "owner", None, None, None),
        check_vma=False,
    )
```

```python
import functools

import jax
import jax.numpy as jnp
from jax import lax
from jax.experimental import pallas as pl
from jax.experimental.pallas import tpu as pltpu
from jax.sharding import PartitionSpec as P

HEAD_DIM = 64
MESH = pl.DeviceIdType.MESH
GROUPS = 1
SIB, UP, DOWN, ACROSS, REGION = range(5)


def padded(value, sides, width):
    for axis, dim in sides:
        devices, length = (lax.axis_size(axis), value.shape[dim])
        up = [(i, (i + 1) % devices) for i in range(devices - 1)]
        down = [(j, i) for i, j in up]
        last = lax.slice_in_dim(value, length - width, length, axis=dim)
        first = lax.slice_in_dim(value, 0, width, axis=dim)
        before = lax.ppermute(last, axis, up)
        after = lax.ppermute(first, axis, down)
        value = jnp.concatenate([before, value, after], axis=dim)
    return value


def layer_norm(inputs, norm_gain):
    widened = inputs.astype(jnp.float32)
    average = jnp.mean(widened, axis=-1, keepdims=True)
    spread = jnp.mean((widened - average) ** 2, axis=-1, keepdims=True)
    return ((widened - average) * lax.rsqrt(spread + 1e-06) * norm_gain).astype(jnp.bfloat16)


def attend_heads(queries, keys, values, bias):
    tokens, pair = queries.shape
    low = lax.broadcasted_iota(jnp.int32, (tokens, pair), 1) < HEAD_DIM
    halves = []
    for mine in (low, jnp.logical_not(low)):
        query = jnp.where(mine, queries, jnp.zeros_like(queries))
        scores = lax.dot_general(
            query, keys, (((1,), (1,)), ((), ())), preferred_element_type=jnp.float32
        ) + bias
        shifted = jnp.exp(scores - jnp.max(scores, axis=-1, keepdims=True))
        total = jnp.sum(shifted, axis=-1, keepdims=True)
        mixed = jnp.dot(shifted.astype(jnp.bfloat16), values, preferred_element_type=jnp.float32)
        halves.append(mixed / total)
    return jnp.where(low, halves[0], halves[1]).astype(jnp.bfloat16)


def fused_kernel(owners, x_ref, wq_ref, wo_ref, gain_ref, bias_ref, out_ref,
                 xs_ref, gq_ref, go_ref, normed_ref, q_ref, kv_ref, mixed_ref,
                 send_q, recv_q, send_o, recv_o, send_x, recv_x, local_sem):
    groups = wq_ref.shape[0]
    share = wq_ref.shape[2] // 3
    tokens, width = x_ref.shape
    others = xs_ref.shape[0]
    planes = owners // 4
    region = lax.axis_index("region")
    owner = lax.axis_index("owner")
    core = lax.rem(owner, 2)
    row = lax.rem(owner // 2, 2)
    plane = owner // 4
    side_owner = owner + 2 * core - 1
    has_side = jnp.logical_and(side_owner >= 0, side_owner < owners)
    has_up = plane < planes - 1
    has_down = plane > 0

    def owner_of(z, y, c):
        return z * 4 + y * 2 + c

    def ident(r, z, y, c):
        return r * owners + owner_of(z, y, c)

    targets = {
        SIB: (region, owner_of(plane, row, 1 - core)),
        UP: (region, owner_of(plane + 1, row, core)),
        DOWN: (region, owner_of(plane - 1, row, core)),
        ACROSS: (region, owner_of(plane, 1 - row, core)),
        REGION: (1 - region, owner),
    }
    conditions = {SIB: None, UP: has_up, DOWN: has_down, ACROSS: None, REGION: None}
    side = (region, side_owner)

    def run(cond, fn):
        if cond is None:
            fn()
        else:
            pl.when(cond)(fn)

    def both(a, b):
        if a is None:
            return b
        return a if b is None else jnp.logical_and(a, b)

    barrier = pltpu.get_barrier_semaphore()

    def greet(target):
        pl.semaphore_signal(barrier, inc=1, device_id=target, device_id_type=MESH)

    for kind, target in targets.items():
        run(conditions[kind], functools.partial(greet, target))
    run(has_side, functools.partial(greet, side))
    pl.semaphore_wait(
        barrier,
        3 + has_up.astype(jnp.int32) + has_down.astype(jnp.int32) + has_side.astype(jnp.int32),
    )

    pending = []

    def start(cond, make):
        run(cond, lambda: make().start())
        pending.append((cond, lambda: make().wait_send()))

    def whole(name):
        return go_ref if name == "o" else gq_ref.at[name]

    def own_shard(name):
        return wo_ref if name == "o" else wq_ref.at[name]

    def rows_of(name, src):
        depth = wo_ref.shape[0]
        return whole(name).at[pl.ds(pl.multiple_of(src * depth, depth), depth), :]

    def send_sem(name, kind, src):
        return send_o.at[kind, src // 2] if name == "o" else send_q.at[name, kind, src // 2]

    def recv_sem(name, src):
        return recv_o.at[src] if name == "o" else recv_q.at[name, src]

    def send(name, kind, src, cond, own=False):
        def make():
            return pltpu.make_async_remote_copy(
                src_ref=own_shard(name) if own else rows_of(name, src),
                dst_ref=rows_of(name, src),
                send_sem=send_sem(name, kind, src),
                recv_sem=recv_sem(name, src),
                device_id=targets[kind],
                device_id_type=MESH,
            )

        start(both(cond, conditions[kind]), make)

    def arrive(name, src, cond):
        def wait():
            pltpu.make_async_remote_copy(
                src_ref=rows_of(name, src),
                dst_ref=rows_of(name, src),
                send_sem=send_sem(name, SIB, src),
                recv_sem=recv_sem(name, src),
                device_id=targets[SIB],
                device_id_type=MESH,
            ).wait_recv()

        run(cond, wait)

    def block_copy(src_ref, slot, target, sem):
        return pltpu.make_async_remote_copy(
            src_ref=src_ref,
            dst_ref=xs_ref.at[slot],
            send_sem=send_x.at[sem],
            recv_sem=recv_x.at[slot],
            device_id=target,
            device_id_type=MESH,
        )

    def send_block(src_ref, slot, target, sem, cond):
        start(cond, lambda: block_copy(src_ref, slot, target, sem))

    def arrive_block(slot, cond):
        run(cond, lambda: block_copy(xs_ref.at[slot], slot, targets[SIB], 0).wait_recv())

    me = ident(region, plane, row, core)

    def at_distance(d):
        if d == 0:
            return [(plane, None, ())]
        return [
            (plane - d, plane - d >= 0, (UP,)),
            (plane + d, plane + d < planes, (DOWN,)),
        ]

    def row_step(g, d):
        for z, cond, _ in at_distance(d):
            src = ident(region, z, 1 - row, core)
            arrive(g, src, cond)
            send(g, REGION, src, cond)
            send(g, SIB, src, cond)

    def plane_step(g, d):
        for z, cond, onward in at_distance(d):
            src = ident(region, z, row, core)
            arrive(g, src, cond)
            for kind in onward + (ACROSS, REGION, SIB):
                send(g, kind, src, cond)

    def own_step(g):
        for kind in (UP, DOWN, ACROSS, REGION, SIB):
            send(g, kind, me, None, own=True)

    def region_step(g, d):
        for y in (row, 1 - row):
            for z, cond, _ in at_distance(d):
                src = ident(1 - region, z, y, core)
                arrive(g, src, cond)
                send(g, SIB, src, cond)

    def sibling_step(name):
        for d in range(planes):
            for r in (region, 1 - region):
                for y in (row, 1 - row):
                    for z, cond, _ in at_distance(d):
                        arrive(name, ident(r, z, y, 1 - core), cond)

    def near_steps(g, own=True):
        steps = [functools.partial(own_step, g)] if own else []
        steps.append(functools.partial(row_step, g, 0))
        for d in range(1, planes):
            steps.append(functools.partial(plane_step, g, d))
            steps.append(functools.partial(row_step, g, d))
        return steps

    def far_steps(g):
        steps = [functools.partial(region_step, g, d) for d in range(planes)]
        return steps + [functools.partial(sibling_step, g)]

    def out_across():
        src = ident(region, plane, 1 - row, core)
        arrive("o", src, None)
        for kind in (REGION, SIB):
            send("o", kind, src, None)

    def out_line():
        for y in (row, 1 - row):
            src = ident(region, plane, y, core)
            for kind in (UP, DOWN):
                send("o", kind, src, None, own=y is row)

    def out_region():
        for y in (row, 1 - row):
            src = ident(1 - region, plane, y, core)
            arrive("o", src, None)
            for kind in (UP, DOWN, SIB):
                send("o", kind, src, None)

    def out_plane(d):
        for r, y in ((region, row), (region, 1 - row), (1 - region, row), (1 - region, 1 - row)):
            for z, cond, onward in at_distance(d):
                src = ident(r, z, y, core)
                arrive("o", src, cond)
                for kind in onward + (SIB,):
                    send("o", kind, src, cond)

    gain = gain_ref[...]

    def norm_block(slot):
        rows = pl.ds(pl.multiple_of((slot + 1) * tokens, tokens), tokens)
        normed_ref[rows, :] = layer_norm(xs_ref[slot], gain)

    bias = bias_ref[...]
    pair = 2 * HEAD_DIM

    def project(g, first, rows):
        kv_ref[first:first + rows, :] = jnp.dot(
            normed_ref[first:first + rows, :], gq_ref[g, :, share:],
            preferred_element_type=jnp.float32,
        ).astype(jnp.bfloat16)

    def project_queries(g):
        part = jnp.dot(
            normed_ref[0:tokens, :], gq_ref[g, :, 0:share], preferred_element_type=jnp.float32
        )
        q_ref[...] = part.astype(jnp.bfloat16) * jnp.bfloat16(HEAD_DIM ** (-0.5))

    def attend_pair(g, at):
        mixed_ref[:, g * share + at:g * share + at + pair] = attend_heads(
            q_ref[:, at:at + pair],
            kv_ref[:, at:at + pair],
            kv_ref[:, share + at:share + at + pair],
            bias,
        )

    def compute_steps(g):
        count = (others + 1) * tokens
        steps = [functools.partial(project_queries, g)]
        steps += [functools.partial(project, g, i, tokens) for i in range(0, count, tokens)]
        return steps + [functools.partial(attend_pair, g, at) for at in range(0, share, pair)]

    def interleave(work, steps):
        done = 0
        for i, piece in enumerate(work):
            piece()
            due = (i + 1) * len(steps) // len(work)
            for step in steps[done:due]:
                step()
            done = due

    for kind in (UP, DOWN, ACROSS):
        send(0, kind, me, None, own=True)
    send_block(x_ref, 4, targets[REGION], 0, None)
    send("o", ACROSS, me, None, own=True)
    send("o", REGION, me, None, own=True)
    for kind in (REGION, SIB):
        send(0, kind, me, None, own=True)
    send("o", SIB, me, None, own=True)
    send_block(x_ref, 1 - core, side, 1, has_side)
    send_block(x_ref, core, targets[SIB], 2, None)
    local = [
        pltpu.make_async_copy(own_shard(name), rows_of(name, me), local_sem.at[i])
        for i, name in enumerate(list(range(groups)) + ["o"])
    ]
    for copy in local:
        copy.start()

    @pl.when(jnp.logical_not(has_side))
    def _():
        xs_ref[core] = jnp.zeros((tokens, width), xs_ref.dtype)
        xs_ref[2 + core] = jnp.zeros((tokens, width), xs_ref.dtype)

    normed_ref[0:tokens, :] = layer_norm(x_ref[...], gain)

    def relay():
        arrive_block(4, None)
        send_block(xs_ref.at[4], 2 + core, targets[SIB], 3, None)
        send_block(xs_ref.at[4], 3 - core, side, 4, has_side)

    def norm_step(slot, cond, wait=True):
        if wait:
            arrive_block(slot, cond)
        norm_block(slot)

    first = near_steps(0, own=False)
    for step in first[:1] + [out_across] + first[1:3] + [relay] + first[3:]:
        step()
    norms = [
        functools.partial(norm_step, 1 - core, None),
        functools.partial(norm_step, 4, None, False),
        functools.partial(norm_step, core, has_side),
        functools.partial(norm_step, 3 - core, None),
        functools.partial(norm_step, 2 + core, has_side),
    ]
    interleave(norms, near_steps(1) if groups > 1 else [])
    for copy in local:
        copy.wait()
    out_line()
    out_region()
    for step in far_steps(0):
        step()
    late = [functools.partial(out_plane, d) for d in range(1, planes)]
    for g in range(groups):
        pieces = compute_steps(g)
        if g == 0:
            middle = len(pieces) // 3
            for piece in pieces[:middle]:
                piece()
            interleave(pieces[middle:], late)
        else:
            for step in far_steps(g):
                step()
            for piece in pieces:
                piece()
        if 0 < g < groups - 1:
            for step in near_steps(g + 1):
                step()
    sibling_step("o")

    tile = min(512, width)
    for at in range(0, width, tile):
        projected = jnp.dot(
            mixed_ref[...], go_ref[:, at:at + tile], preferred_element_type=jnp.float32
        )
        out_ref[:, at:at + tile] = (
            x_ref[:, at:at + tile].astype(jnp.float32) + projected
        ).astype(out_ref.dtype)
    for cond, wait in pending:
        run(cond, wait)


def fused(block, qkv_weight, out_weight, norm_gain, bias):
    owners = lax.axis_size("owner")
    devices = lax.axis_size("region") * owners
    tokens, width = block.shape
    depth = qkv_weight.shape[0]
    groups = GROUPS
    share = width // groups
    parted = qkv_weight.reshape(depth, 3, groups, share).transpose(2, 0, 1, 3)
    parted = parted.reshape(groups, depth, 3 * share)
    count = bias.shape[1]
    vmem = pl.BlockSpec(memory_space=pltpu.VMEM)
    return pl.pallas_call(
        functools.partial(fused_kernel, owners),
        out_shape=jax.ShapeDtypeStruct(block.shape, block.dtype),
        in_specs=[vmem] * 5,
        out_specs=vmem,
        scratch_shapes=[
            pltpu.VMEM((5, tokens, width), block.dtype),
            pltpu.VMEM((groups, devices * depth, 3 * share), qkv_weight.dtype),
            pltpu.VMEM((devices * depth, width), out_weight.dtype),
            pltpu.VMEM((count, width), jnp.bfloat16),
            pltpu.VMEM((tokens, share), jnp.bfloat16),
            pltpu.VMEM((count, 2 * share), jnp.bfloat16),
            pltpu.VMEM((tokens, width), jnp.bfloat16),
            pltpu.SemaphoreType.DMA((groups, 5, devices // 2)),
            pltpu.SemaphoreType.DMA((groups, devices)),
            pltpu.SemaphoreType.DMA((5, devices // 2)),
            pltpu.SemaphoreType.DMA((devices,)),
            pltpu.SemaphoreType.DMA((5,)),
            pltpu.SemaphoreType.DMA((5,)),
            pltpu.SemaphoreType.DMA((groups + 1,)),
        ],
        compiler_params=pltpu.CompilerParams(
            collective_id=0, has_side_effects=True, vmem_limit_bytes=60 * 1024 * 1024
        ),
        name="fused",
    )(block, parted, out_weight, norm_gain, bias)


def attend_kernel(listed_ref, x_ref, xs_ref, gain_ref, bias_ref, wq_ref, wo_ref, out_ref,
                  normed_ref, q_ref, kv_ref, mixed_ref):
    tokens, width = x_ref.shape
    others = xs_ref.shape[0]
    gain = gain_ref[...]
    normed_ref[0:tokens, :] = layer_norm(x_ref[...], gain)

    @pl.loop(0, others)
    def _(slot):
        rows = pl.ds(pl.multiple_of((slot + 1) * tokens, tokens), tokens)
        block = xs_ref[slot].astype(jnp.float32)
        block = jnp.where(listed_ref[slot] > 0, block, 0.0)
        normed_ref[rows, :] = layer_norm(block, gain)

    tile = min(512, width)

    @pl.loop(0, width // tile)
    def _(step):
        cols = pl.ds(pl.multiple_of(step * tile, tile), tile)
        part = jnp.dot(normed_ref[0:tokens, :], wq_ref[:, cols], preferred_element_type=jnp.float32)
        q_ref[:, cols] = part.astype(jnp.bfloat16) * jnp.bfloat16(HEAD_DIM ** (-0.5))

    @pl.loop(0, 2 * width // tile)
    def _(step):
        cols = pl.ds(pl.multiple_of(step * tile, tile), tile)
        from_cols = pl.ds(pl.multiple_of(width + step * tile, tile), tile)
        kv_ref[:, cols] = jnp.dot(
            normed_ref[...], wq_ref[:, from_cols], preferred_element_type=jnp.float32
        ).astype(jnp.bfloat16)

    pair = 2 * HEAD_DIM
    low = lax.broadcasted_iota(jnp.int32, (tokens, pair), 1) < HEAD_DIM
    bias = bias_ref[...]

    @pl.loop(0, width // pair)
    def _(group):
        cols = pl.ds(pl.multiple_of(group * pair, pair), pair)
        value_cols = pl.ds(pl.multiple_of(width + group * pair, pair), pair)
        queries = q_ref[:, cols]
        keys = kv_ref[:, cols]
        values = kv_ref[:, value_cols]
        halves = []
        for mine in (low, jnp.logical_not(low)):
            query = jnp.where(mine, queries, jnp.zeros_like(queries))
            scores = lax.dot_general(
                query, keys, (((1,), (1,)), ((), ())), preferred_element_type=jnp.float32
            ) + bias
            shifted = jnp.exp(scores - jnp.max(scores, axis=-1, keepdims=True))
            total = jnp.sum(shifted, axis=-1, keepdims=True)
            mixed = jnp.dot(shifted.astype(jnp.bfloat16), values, preferred_element_type=jnp.float32)
            halves.append(mixed / total)
        mixed_ref[:, cols] = jnp.where(low, halves[0], halves[1]).astype(jnp.bfloat16)

    @pl.loop(0, width // tile)
    def _(step):
        cols = pl.ds(pl.multiple_of(step * tile, tile), tile)
        projected = jnp.dot(mixed_ref[...], wo_ref[:, cols], preferred_element_type=jnp.float32)
        out_ref[:, cols] = (x_ref[:, cols].astype(jnp.float32) + projected).astype(out_ref.dtype)


def attend(listed, block, others, norm_gain, bias, qkv_weight, out_weight):
    tokens, width = block.shape
    count = (others.shape[0] + 1) * tokens
    vmem = pl.BlockSpec(memory_space=pltpu.VMEM)
    return pl.pallas_call(
        attend_kernel,
        out_shape=jax.ShapeDtypeStruct(block.shape, block.dtype),
        in_specs=[pl.BlockSpec(memory_space=pltpu.SMEM)] + [vmem] * 6,
        out_specs=vmem,
        scratch_shapes=[
            pltpu.VMEM((count, width), jnp.bfloat16),
            pltpu.VMEM((tokens, width), jnp.bfloat16),
            pltpu.VMEM((count, 2 * width), jnp.bfloat16),
            pltpu.VMEM((tokens, width), jnp.bfloat16),
        ],
        compiler_params=pltpu.CompilerParams(vmem_limit_bytes=60 * 1024 * 1024),
        name="attend",
    )(listed, block, others, norm_gain, bias, qkv_weight, out_weight)


def shards(voxels, norm_gain, qkv_weight, out_weight, neighbours):
    block_size, model_width = voxels.shape[-2:]
    block = voxels.reshape(block_size, model_width)
    regions, owners = (lax.axis_size("region"), lax.axis_size("owner"))
    region, owner = (lax.axis_index("region"), lax.axis_index("owner"))
    together = regions == 2 and owners % 4 == 0 and owners > 4
    if together:
        offsets = [(0, -1), (0, 1), (1 - 2 * region, -1), (1 - 2 * region, 1), (1 - 2 * region, 0)]
    else:
        wide = padded(voxels[:, :, 0], (("owner", 1), ("region", 0)), 1)
        wide = wide.reshape(-1, block_size, model_width)
        middle = wide.shape[0] // 2
        others = jnp.concatenate([wide[:middle], wide[middle + 1:]], axis=0)
        full_qkv = lax.all_gather(qkv_weight, ("region", "owner"), axis=0, tiled=True)
        full_out = lax.all_gather(out_weight, ("region", "owner"), axis=0, tiled=True)
        offsets = [(i, j) for i in (-1, 0, 1) for j in (-1, 0, 1) if i or j]
    numbers = []
    for up, along in offsets:
        inside = (owner + along >= 0) & (owner + along < owners)
        number = (region + up) * owners + owner + along
        numbers.append(jnp.where(inside & (number >= 0), number, -2))
    listed = jnp.any(neighbours.reshape(1, -1) == jnp.stack(numbers)[:, None], axis=1)
    present = jnp.concatenate([jnp.ones((1,), bool), listed])
    bias = jnp.repeat(jnp.where(present, 0.0, -1e30).astype(jnp.float32), block_size)[None, :]
    if together:
        out = fused(block, qkv_weight, out_weight, norm_gain[None, :], bias)
        return out.reshape(voxels.shape)
    out = attend(
        listed.astype(jnp.int32), block, others, norm_gain[None, :], bias, full_qkv, full_out
    )
    return out.reshape(voxels.shape)


def solution(mesh):
    return jax.shard_map(
        shards,
        mesh=mesh,
        in_specs=(
            P("region", "owner", None, None, None),
            P(),
            P(("region", "owner"), None),
            P(("region", "owner"), None),
            P("region", "owner", None, None),
        ),
        out_specs=P("region", "owner", None, None, None),
        check_vma=False,
    )
```
